32 devices in a mesh: dp: 8 (over y, x, core), tensor: 4 (over z).
Axes of the slice: x: 2, y: 2, z: 4, core: 2. Of those that a mesh axis runs over, the one named last changes fastest.
Arguments:
- block_input: bfloat16 [8192, 2560], P(('dp', 'tensor')), may hold values from -6 to 6
- segment_ids: int32 [8, 1024], P('dp'), may hold values from 0 to 2, never falling along the last dimension, each value on 1 to 512 neighbouring positions
- output_cotangent: bfloat16 [8192, 2560], P(('dp', 'tensor')), may hold values from -6 to 6
- first_gain: bfloat16 [2560], replicated, may hold values from 0.25 to 1.75
- input_weight: bfloat16 [2560, 2560], P('dp', 'tensor'), may hold values from -0.125 to 0.125
- gelu_weight: bfloat16 [2560, 2560], P('dp', 'tensor'), may hold values from -0.125 to 0.125
- conv_kernel: bfloat16 [4, 2560], P(None, 'tensor'), may hold values from -3 to 3
- conv_bias: bfloat16 [2560], P('tensor'), may hold values from -3 to 3
- alpha_weight: bfloat16 [8, 320, 320], P('tensor'), may hold values from -0.3125 to 0.3125
- alpha_bias: bfloat16 [2560], P('tensor'), may hold values from -4 to 4
- update_weight: bfloat16 [8, 320, 320], P('tensor'), may hold values from -0.3125 to 0.3125
- update_bias: bfloat16 [2560], P('tensor'), may hold values from -4 to 4
- decay_param: bfloat16 [2560], P('tensor'), may hold values from -9 to -1
- mixer_weight: bfloat16 [2560, 2560], P('tensor', 'dp'), may hold values from -0.125 to 0.125
- second_gain: bfloat16 [2560], replicated, may hold values from 0.25 to 1.75
- gate_weight: bfloat16 [2560, 7680], P('dp', 'tensor'), may hold values from -0.125 to 0.125
- up_weight: bfloat16 [2560, 7680], P('dp', 'tensor'), may hold values from -0.125 to 0.125
- down_weight: bfloat16 [7680, 2560], P('tensor', 'dp'), may hold values from -0.0625 to 0.0625
Outputs:
- block_output: bfloat16 [8192, 2560], P(('dp', 'tensor'))
- input_grad: float32 [8192, 2560], P(('dp', 'tensor'))
- grad_first_gain: float32 [2560], replicated
- grad_input_weight: float32 [2560, 2560], P('dp', 'tensor')
- grad_gelu_weight: float32 [2560, 2560], P('dp', 'tensor')
- grad_conv_kernel: float32 [4, 2560], P(None, 'tensor')
- grad_conv_bias: float32 [2560], P('tensor')
- grad_alpha_weight: float32 [8, 320, 320], P('tensor')
- grad_alpha_bias: float32 [2560], P('tensor')
- grad_update_weight: float32 [8, 320, 320], P('tensor')
- grad_update_bias: float32 [2560], P('tensor')
- grad_decay_param: float32 [2560], P('tensor')
- grad_mixer_weight: float32 [2560, 2560], P('tensor', 'dp')
- grad_second_gain: float32 [2560], replicated
- grad_gate_weight: float32 [2560, 7680], P('dp', 'tensor')
- grad_up_weight: float32 [2560, 7680], P('dp', 'tensor')
- grad_down_weight: float32 [7680, 2560], P('tensor', 'dp')
The draws below stay inside these ranges and needn't reach their ends.
Inputs may be any that keep to these rules, and one draw needn't show every extreme that they name: `segment_ids`: along each sequence of 1024 tokens the numbers never fall; a document starts at the first token and wherever the number changes; a document has at most 512 tokens.
All inputs are finite; a program needn't handle non-finite values.
Results may differ from the reference program's by a relative error of at most 0.0087.
Values may be sent and summed in bfloat16 or wider, within the bound.
A program may use at most 320 MiB of HBM per device.

```python
import math
import jax
import jax.numpy as jnp
import numpy as np
from jax import lax

D = 2560
LRU = 2560
FF = 7680
BLOCKS = 8
CONV = 4
LEN = 1024
SEG_N = 3
BW = 320
SEQS = 8
TOKENS = 8192


def levels(stream_key, extent, shards, low, high):
    loudness, own = 1.0, jax.random.fold_in(stream_key, 6)
    for position, parts in shards:
        draws = jnp.exp(jax.random.uniform(jax.random.fold_in(own, position), (parts,), jnp.float32, low / len(shards), high / len(shards)))
        loudness = loudness * jnp.repeat(draws, extent[position] // parts).reshape([-1 if axis == position else 1 for axis in range(len(extent))])
    return loudness


def split_up(number_of, total, most, lean):
    weights = [(1 << 20) // math.isqrt(standing ** lean) + 1 for standing in range(2, number_of + 1)]
    spare, given = total - most - (number_of - 1), [1] * (number_of - 1)
    while spare > 0:
        candidates = [i for i in range(number_of - 1) if given[i] < most]
        whole, left = sum([weights[i] for i in candidates]), spare
        for i in candidates:
            extra = min(most - given[i], max(1, left * weights[i] // whole), spare)
            given[i] = given[i] + extra
            spare = spare - extra
    return np.array([most] + given)


def uneven_parts(rng, count, total, limit, slope):
    if count == 2:
        one = jax.random.randint(rng, (), max(1, total - limit), min(limit, total - 1) + 1)
        return jnp.stack([one, total - one])
    sizes = jnp.asarray(split_up(count, total, limit, slope), jnp.int32)
    twos = (count - 1) // 2
    donor, taker = sizes[1:1 + 2 * twos:2], sizes[2:2 + 2 * twos:2]
    room = jnp.minimum(donor - 1, limit - taker)
    passed = jax.random.randint(jax.random.fold_in(rng, 1), (twos,), 0, 1 << 20) % (room + 1)
    sizes = sizes.at[1:1 + 2 * twos:2].set(donor - passed).at[2:2 + 2 * twos:2].set(taker + passed)
    return sizes[jax.random.permutation(jax.random.fold_in(rng, 2), count)]


def gaussian(rng, extent, scale, reach, shards=(), dtype=jnp.bfloat16):
    array = jax.random.normal(rng, extent, jnp.float32) * scale
    if len(shards) > 0:
        array = levels(rng, extent, shards, -0.22, 0.18) * array
    return jnp.clip(array, min=-reach, max=reach).astype(dtype)


def setup_inputs(seed: int = 0) -> dict:
    key_of = jax.random.split(jax.random.key(seed), 19)
    return {
        "block_input": gaussian(key_of[0], (TOKENS, D), 1.0, 6.0, ((0, 32),)),
        "segment_ids": jax.vmap(lambda own: jnp.searchsorted(jnp.cumsum(uneven_parts(own, SEG_N, LEN, LEN // 2, 1)), jnp.arange(LEN), side="right"))(jax.random.split(key_of[1], SEQS)).reshape((SEQS, LEN)).astype(jnp.int32),
        "output_cotangent": gaussian(key_of[2], (TOKENS, D), 1.0, 6.0, ((0, 32),)),
        "first_gain": jnp.clip(1.0 + 0.15 * jax.random.normal(key_of[3], (D,), jnp.float32), 0.25, 1.75).astype(jnp.bfloat16),
        "input_weight": gaussian(key_of[4], (D, LRU), D ** -0.5, 0.125, ((0, 8), (1, 4))),
        "gelu_weight": gaussian(key_of[5], (D, LRU), D ** -0.5, 0.125, ((0, 8), (1, 4))),
        "conv_kernel": gaussian(key_of[6], (CONV, LRU), 0.5, 3.0, ((1, 4),)),
        "conv_bias": gaussian(key_of[7], (LRU,), 0.5, 3.0, ((0, 4),)),
        "alpha_weight": gaussian(key_of[8], (BLOCKS, BW, BW), BW ** -0.5, 0.3125, ((0, 4),)),
        "alpha_bias": gaussian(key_of[9], (LRU,), 1.0, 4.0, ((0, 4),)),
        "update_weight": gaussian(key_of[10], (BLOCKS, BW, BW), BW ** -0.5, 0.3125, ((0, 4),)),
        "update_bias": gaussian(key_of[11], (LRU,), 1.0, 4.0, ((0, 4),)),
        "decay_param": jnp.clip(-9.0 + 8.0 * jax.random.uniform(key_of[12], (LRU,), jnp.float32) ** levels(key_of[12], (LRU,), ((0, 4),), -0.2, 0.2), -9.0, -1.0).astype(jnp.bfloat16),
        "mixer_weight": gaussian(key_of[13], (LRU, D), LRU ** -0.5, 0.125, ((0, 4), (1, 8))),
        "second_gain": jnp.clip(1.0 + 0.15 * jax.random.normal(key_of[14], (D,), jnp.float32), 0.25, 1.75).astype(jnp.bfloat16),
        "gate_weight": gaussian(key_of[15], (D, FF), D ** -0.5, 0.125, ((0, 8), (1, 4))),
        "up_weight": gaussian(key_of[16], (D, FF), D ** -0.5, 0.125, ((0, 8), (1, 4))),
        "down_weight": gaussian(key_of[17], (FF, D), FF ** -0.5, 0.0625, ((0, 4), (1, 8))),
    }


EPSILON = 1e-06
RATE_SCALE = 8.0
HIGHEST = lax.Precision.HIGHEST

@jax.custom_vjp
def low(v):
    return lax.optimization_barrier(v.astype(jnp.bfloat16)).astype(jnp.float32)

@jax.custom_vjp
def low_back(v):
    return v

def low_keep(v):
    return (low(v), None)

def low_pass(kept, grad):
    return (grad,)

def back_keep(v):
    return (v, None)

def back_low(kept, grad):
    return (low(grad),)
low.defvjp(low_keep, low_pass)
low_back.defvjp(back_keep, back_low)

def matmul(left, right):
    return jnp.dot(left, right, precision=HIGHEST, preferred_element_type=jnp.float32)

def norm_rows(values, gain):
    inverse = lax.rsqrt(lax.optimization_barrier(jnp.mean(values * values, axis=-1, keepdims=True)) + EPSILON)
    return values * inverse * gain

def delayed(values, offset):
    filler = jnp.zeros_like(values[:offset])
    return jnp.concatenate([filler, values[:values.shape[0] - offset]], axis=0)

def recurrence_inputs(keeping, conv_out, alpha_pre, update_pre, decay_param):
    alpha_gate = jax.nn.sigmoid(alpha_pre)
    update_gate = jax.nn.sigmoid(update_pre)
    log_decay = -RATE_SCALE * alpha_gate * jax.nn.softplus(decay_param)
    scaling = keeping * jnp.sqrt(-jnp.expm1(2.0 * log_decay)) + (1.0 - keeping)
    return (keeping * jnp.exp(log_decay), conv_out * update_gate * scaling)

def advance(state, pair):
    state = pair[0] * state + pair[1]
    return (state, state)

def sequence_forward(segment, tokens, params):
    first_gain, input_weight, gelu_weight, conv_kernel, conv_bias, alpha_weight, alpha_bias, update_weight, update_bias, decay_param, mixer_weight, second_gain, gate_weight, up_weight, down_weight = params
    length = tokens.shape[0]
    same_doc = [None]
    for offset in range(1, CONV):
        earlier = jnp.concatenate([jnp.full((offset,), -1, jnp.int32), segment[:length - offset].astype(jnp.int32)])
        same_doc.append((earlier == segment.astype(jnp.int32)).astype(jnp.float32)[:, None])
    keeping = same_doc[1]
    normed = low(norm_rows(tokens, first_gain))
    branch = low_back(matmul(normed, input_weight))
    gate_pre = low_back(matmul(normed, gelu_weight))
    gelu_out = jax.nn.gelu(gate_pre, approximate=True)
    conv_sum = branch * conv_kernel[0] + conv_bias
    for offset in range(1, CONV):
        conv_sum = conv_sum + delayed(branch, offset) * same_doc[offset] * conv_kernel[offset]
    conv_out = low(conv_sum)
    grouped = conv_out.reshape(length, BLOCKS, BW)
    alpha_pre = low_back(jnp.einsum('tbi,bij->tbj', grouped, alpha_weight, precision=HIGHEST).reshape(length, LRU) + alpha_bias)
    update_pre = low_back(jnp.einsum('tbi,bij->tbj', grouped, update_weight, precision=HIGHEST).reshape(length, LRU) + update_bias)
    decay, driven = recurrence_inputs(keeping, conv_out, alpha_pre, update_pre, decay_param)
    _, states = lax.scan(advance, jnp.zeros((LRU,), jnp.float32), (decay, driven))
    mixed = low(states * gelu_out)
    branch_out = low_back(matmul(mixed, mixer_weight))
    middle = tokens + branch_out
    second = low(norm_rows(middle, second_gain))
    gate_vals = low_back(matmul(second, gate_weight))
    up_vals = low_back(matmul(second, up_weight))
    hidden = low(jax.nn.gelu(gate_vals, approximate=True) * up_vals)
    ffw_out = low_back(matmul(hidden, down_weight))
    return middle + ffw_out

def add_trees(first_tree, second_tree):
    return jax.tree.map(jnp.add, first_tree, second_tree)

def reference(block_input, segment_ids, output_cotangent, first_gain, input_weight, gelu_weight, conv_kernel, conv_bias, alpha_weight, alpha_bias, update_weight, update_bias, decay_param, mixer_weight, second_gain, gate_weight, up_weight, down_weight):
    raw_params = (first_gain, input_weight, gelu_weight, conv_kernel, conv_bias, alpha_weight, alpha_bias, update_weight, update_bias, decay_param, mixer_weight, second_gain, gate_weight, up_weight, down_weight)
    params = tuple((single.astype(jnp.float32) for single in raw_params))
    inputs = block_input.astype(jnp.float32).reshape(SEQS, LEN, D)
    cotangents = output_cotangent.astype(jnp.float32).reshape(SEQS, LEN, D)

    def per_sequence(totals, item):
        tokens, segment, cotangent = item
        result, pullback = jax.vjp(partial_forward(segment), tokens, params)
        token_grad, param_grads = pullback(cotangent)
        return (add_trees(totals, param_grads), (result, token_grad))
    zeros = jax.tree.map(jnp.zeros_like, params)
    totals, (results, token_grads) = lax.scan(per_sequence, zeros, (inputs, segment_ids, cotangents))
    return (results.reshape(TOKENS, D).astype(jnp.bfloat16), token_grads.reshape(TOKENS, D), totals[0], totals[1], totals[2], totals[3], totals[4], totals[5], totals[6], totals[7], totals[8], totals[9], totals[10], totals[11], totals[12], totals[13], totals[14])

def partial_forward(segment):

    def forward(tokens, params):
        return sequence_forward(segment, tokens, params)
    return forward
```

```python
from functools import partial

import jax
import jax.numpy as jnp
from jax import lax
from jax.experimental import pallas as pl
from jax.experimental.pallas import tpu as pltpu
from jax.sharding import PartitionSpec as P

EPSILON = 1e-06
RATE_SCALE = 8.0
GELU_C = 0.7978845608028654
GELU_A = 0.044715
GROUP = 8

F32 = jnp.float32
BF16 = jnp.bfloat16


def norm_rows(values, gain):
    inverse = lax.rsqrt(jnp.mean(values * values, axis=-1, keepdims=True) + EPSILON)
    return values * inverse * gain


def gated_hidden(gate_vals, up_vals):
    return jax.nn.gelu(gate_vals, approximate=True) * up_vals


def matmul(left, right):
    return jnp.dot(left, right, preferred_element_type=F32)


def inner_rows(left, right):
    return lax.dot_general(left, right, (((0,), (0,)), ((), ())), preferred_element_type=F32)


def times_transposed(left, right):
    return lax.dot_general(left, right, (((1,), (1,)), ((), ())), preferred_element_type=F32)


def mask_table(segment, taps):
    length = segment.shape[0]
    same, ahead = [], []
    for offset in range(1, taps):
        equal = (segment[offset:] == segment[:-offset]).astype(F32)
        same.append(jnp.pad(equal, (offset, 0)))
        ahead.append(jnp.pad(equal, (0, offset)))
    table = jnp.stack(same + ahead, axis=1)
    return jnp.pad(table, ((0, 0), (0, 8 - table.shape[1])))


def gelu_parts(v):
    th = jnp.tanh(GELU_C * (v + GELU_A * (v * v * v)))
    return 0.5 * (1.0 + th), th


def gate_terms(conv_f, pre, rate, keep, channels):
    alpha = jax.nn.sigmoid(pre[:, :channels])
    update = jax.nn.sigmoid(pre[:, channels:])
    log_decay = -rate * alpha
    th = jnp.tanh(log_decay)
    gap = (-2.0 * th) / (1.0 - th)
    return alpha, update, jnp.exp(log_decay), gap


def group_scan(a, b, reverse):
    rows, channels = a.shape
    a = a.reshape(rows // GROUP, GROUP, channels)
    b = b.reshape(rows // GROUP, GROUP, channels)
    place = lax.broadcasted_iota(jnp.int32, a.shape, 1)
    shift = 1
    while shift < GROUP:
        if reverse:
            inside = place < GROUP - shift
            step = GROUP - shift
        else:
            inside = place >= shift
            step = shift
        b_far = jnp.where(inside, pltpu.roll(b, step, 1), 0.0)
        a_far = jnp.where(inside, pltpu.roll(a, step, 1), 1.0)
        b = a * b_far + b
        a = a * a_far
        shift *= 2
    return a.reshape(rows, channels), b.reshape(rows, channels)


def forward_kernel(
    order, bg, table, taps, conv_bias, gate_w, gate_b, rate, mixed, states, conv_low, ext, carry, a_s, b_s
):
    step = pl.program_id(0)
    rows, channels = states.shape[1], states.shape[2]

    @pl.when(step == 0)
    def _():
        ext[0:8, :] = jnp.zeros((8, channels), F32)
        carry[...] = jnp.zeros((8, channels), F32)

    branch = bg[0, :, :channels]
    ext[8 : 8 + rows, :] = branch
    conv = branch * taps[0:1, :] + conv_bias[...]
    for k in range(1, 4):
        conv = conv + ext[8 - k : 8 - k + rows, :] * table[:, k - 1 : k] * taps[k : k + 1, :]
    ext[0:8, :] = ext[rows : rows + 8, :]
    low = conv.astype(BF16)
    conv_low[0] = low
    pre = matmul(low, gate_w[...]) + gate_b[...]
    keep = table[:, 0:1]
    conv_f = low.astype(F32)
    alpha, update, e, gap = gate_terms(conv_f, pre, rate[...], keep, channels)
    driven = conv_f * update * (keep * jnp.sqrt(gap) + (1.0 - keep))
    a, b = group_scan(keep * e, driven, False)
    a_s[...] = a
    b_s[...] = b

    def advance(g, held):
        at = pl.ds(pl.multiple_of(g * GROUP, GROUP), GROUP)
        now = a_s[at, :] * held + b_s[at, :]
        b_s[at, :] = now
        return jnp.broadcast_to(now[GROUP - 1 : GROUP, :], (GROUP, channels))

    carry[...] = lax.fori_loop(0, rows // GROUP, advance, carry[...], unroll=4)
    state = b_s[...]
    states[0] = state
    gate = bg[0, :, channels:]
    half, _ = gelu_parts(gate)
    mixed[0] = (state * (gate * half)).astype(BF16)


def recurrent_forward(order, bg, table, taps, conv_bias, gate_w, gate_b, rate):
    parts, rows, wide = bg.shape
    channels = wide // 2
    spun = lambda i, o: (o[i], 0, 0)
    whole = lambda i, o: (0, 0)
    return pl.pallas_call(
        forward_kernel,
        grid_spec=pltpu.PrefetchScalarGridSpec(
            num_scalar_prefetch=1,
            grid=(parts,),
            in_specs=[
                pl.BlockSpec((1, rows, wide), spun),
                pl.BlockSpec((rows, 8), lambda i, o: (i, 0)),
                pl.BlockSpec(taps.shape, whole),
                pl.BlockSpec(conv_bias.shape, whole),
                pl.BlockSpec(gate_w.shape, whole),
                pl.BlockSpec(gate_b.shape, whole),
                pl.BlockSpec(rate.shape, whole),
            ],
            out_specs=[
                pl.BlockSpec((1, rows, channels), spun),
                pl.BlockSpec((1, rows, channels), spun),
                pl.BlockSpec((1, rows, channels), spun),
            ],
            scratch_shapes=[
                pltpu.VMEM((rows + 8, channels), F32),
                pltpu.VMEM((8, channels), F32),
                pltpu.VMEM((rows, channels), F32),
                pltpu.VMEM((rows, channels), F32),
            ],
        ),
        out_shape=[
            jax.ShapeDtypeStruct((parts, rows, channels), BF16),
            jax.ShapeDtypeStruct((parts, rows, channels), F32),
            jax.ShapeDtypeStruct((parts, rows, channels), BF16),
        ],
        compiler_params=pltpu.CompilerParams(
            dimension_semantics=("arbitrary",), vmem_limit_bytes=48 << 20
        ),
        cost_estimate=pl.CostEstimate(
            flops=parts * rows * channels * (4 * channels + 200),
            bytes_accessed=parts * rows * channels * 16,
            transcendentals=parts * rows * channels * 6,
        ),
        name="recurrent_forward",
    )(order, bg, table, taps, conv_bias, gate_w, gate_b, rate)


def rows_to_groups(values):
    rows, channels = values.shape
    return jnp.sum(values.reshape(rows // GROUP, GROUP, channels), axis=0)


def backward_kernel(
    order, d_mixed, bg, before_bg, state_in, before_state, conv_low, table, taps, gate_w, gate_b, rate,
    d_bg, grad_w, sums, bias_sums, ext, shifted, carry, d_head, a_s, b_s,
):
    step = pl.program_id(0)
    rows, channels = state_in.shape[1], state_in.shape[2]

    @pl.when(step == 0)
    def _():
        carry[...] = jnp.zeros(carry.shape, F32)
        d_head[...] = jnp.zeros(d_head.shape, F32)
        grad_w[...] = jnp.zeros(grad_w.shape, F32)
        sums[...] = jnp.zeros(sums.shape, F32)
        bias_sums[...] = jnp.zeros(bias_sums.shape, F32)

    keep = table[:, 0:1]
    low = conv_low[0]
    conv_f = low.astype(F32)
    pre = matmul(low, gate_w[...]) + gate_b[...]
    alpha, update, e, gap = gate_terms(conv_f, pre, rate[...], keep, channels)
    root = jnp.sqrt(gap)
    scaling = keep * root + (1.0 - keep)
    decay = keep * e
    gate = bg[0, :, channels:]
    half, th = gelu_parts(gate)
    slope = half + 0.5 * gate * (1.0 - th * th) * (GELU_C * (1.0 + 3.0 * GELU_A * (gate * gate)))
    state = state_in[0]
    d_mix = d_mixed[0]
    d_state = d_mix * (gate * half)
    d_bg[0, :, channels:] = (d_mix * state * slope).astype(BF16)

    shifted[0:rows, :] = decay
    shifted[rows : rows + 8, :] = jnp.ones((8, channels), F32)
    a, b = group_scan(shifted[1 : 1 + rows, :], d_state, True)
    a_s[...] = a
    b_s[...] = b
    groups = rows // GROUP

    def advance(g, held):
        at = pl.ds(pl.multiple_of((groups - 1 - g) * GROUP, GROUP), GROUP)
        now = b_s[at, :] + a_s[at, :] * held
        b_s[at, :] = now
        return jnp.broadcast_to(now[0:1, :], (GROUP, channels))

    first = lax.fori_loop(0, groups, advance, carry[...], unroll=4)
    carry[...] = jnp.broadcast_to(decay[0:1, :], (GROUP, channels)) * first
    adjoint = b_s[...]

    ext[0:8, :] = before_state[0]
    ext[8 : 8 + rows, :] = state
    d_decay = adjoint * ext[7 : 7 + rows, :]
    d_direct = adjoint * update * scaling
    d_update = adjoint * conv_f * scaling * (update * (1.0 - update))
    d_log = keep * (e * d_decay - adjoint * conv_f * update * (e * e / root))
    by_rate = alpha * d_log
    d_alpha = -rate[...] * (by_rate * (1.0 - alpha))
    d_pre = jnp.concatenate([d_alpha, d_update], axis=1).astype(BF16)
    grad_w[...] += inner_rows(low, d_pre)
    bias_sums[...] += rows_to_groups(d_pre.astype(F32))
    d_conv = d_direct + times_transposed(d_pre, gate_w[...])

    ext[0:8, :] = before_bg[0, :, :channels]
    ext[8 : 8 + rows, :] = bg[0, :, :channels]
    shifted[0:rows, :] = d_conv
    shifted[rows : rows + 8, :] = d_head[...]
    d_head[...] = d_conv[0:8, :]
    d_branch = d_conv * taps[0:1, :]
    sums[0] += rows_to_groups(d_conv * ext[8 : 8 + rows, :])
    for k in range(1, 4):
        sums[k] += rows_to_groups(d_conv * (ext[8 - k : 8 - k + rows, :] * table[:, k - 1 : k]))
        d_branch = d_branch + shifted[k : k + rows, :] * table[:, 2 + k : 3 + k] * taps[k : k + 1, :]
    sums[4] += rows_to_groups(d_conv)
    sums[5] += rows_to_groups(by_rate)
    d_bg[0, :, :channels] = d_branch.astype(BF16)


def recurrent_backward(order, d_mixed, bg, states, conv_low, table, taps, gate_w, gate_b, rate):
    parts, rows, wide = bg.shape
    channels = wide // 2
    last = rows // 8 - 1
    spun = lambda i, o: (o[parts - 1 - i], 0, 0)
    before = lambda i, o: (o[jnp.maximum(parts - 2 - i, 0)], last, 0)
    whole = lambda i, o: (0, 0)
    whole3 = lambda i, o: (0, 0, 0)
    return pl.pallas_call(
        backward_kernel,
        grid_spec=pltpu.PrefetchScalarGridSpec(
            num_scalar_prefetch=1,
            grid=(parts,),
            in_specs=[
                pl.BlockSpec((1, rows, channels), spun),
                pl.BlockSpec((1, rows, wide), spun),
                pl.BlockSpec((1, 8, wide), before),
                pl.BlockSpec((1, rows, channels), spun),
                pl.BlockSpec((1, 8, channels), before),
                pl.BlockSpec((1, rows, channels), spun),
                pl.BlockSpec((rows, 8), lambda i, o: (parts - 1 - i, 0)),
                pl.BlockSpec(taps.shape, whole),
                pl.BlockSpec(gate_w.shape, whole),
                pl.BlockSpec(gate_b.shape, whole),
                pl.BlockSpec(rate.shape, whole),
            ],
            out_specs=[
                pl.BlockSpec((1, rows, wide), spun),
                pl.BlockSpec((channels, wide), whole),
                pl.BlockSpec((6, 8, channels), whole3),
                pl.BlockSpec((8, wide), whole),
            ],
            scratch_shapes=[
                pltpu.VMEM((rows + 8, channels), F32),
                pltpu.VMEM((rows + 8, channels), F32),
                pltpu.VMEM((8, channels), F32),
                pltpu.VMEM((8, channels), F32),
                pltpu.VMEM((rows, channels), F32),
                pltpu.VMEM((rows, channels), F32),
            ],
        ),
        out_shape=[
            jax.ShapeDtypeStruct((parts, rows, wide), BF16),
            jax.ShapeDtypeStruct((channels, wide), F32),
            jax.ShapeDtypeStruct((6, 8, channels), F32),
            jax.ShapeDtypeStruct((8, wide), F32),
        ],
        compiler_params=pltpu.CompilerParams(
            dimension_semantics=("arbitrary",), vmem_limit_bytes=48 << 20
        ),
        cost_estimate=pl.CostEstimate(
            flops=parts * rows * channels * (12 * channels + 300),
            bytes_accessed=parts * rows * channels * 24,
            transcendentals=parts * rows * channels * 6,
        ),
        name="recurrent_backward",
    )(order, d_mixed, bg, bg, states, states, conv_low, table, taps, gate_w, gate_b, rate)


def block_diagonal(weight):
    blocks, width, _ = weight.shape
    rows = [
        jnp.pad(weight[b], ((0, 0), (b * width, (blocks - 1 - b) * width))) for b in range(blocks)
    ]
    return jnp.concatenate(rows, axis=0)


def body(
    parts,
    block_input,
    segment_ids,
    output_cotangent,
    first_gain,
    input_weight,
    gelu_weight,
    conv_kernel,
    conv_bias,
    alpha_weight,
    alpha_bias,
    update_weight,
    update_bias,
    decay_param,
    mixer_weight,
    second_gain,
    gate_weight,
    up_weight,
    down_weight,
):
    rows = block_input.shape[0]
    channels = input_weight.shape[1]
    units = gate_weight.shape[1]
    blocks, block_width = alpha_weight.shape[0], alpha_weight.shape[1]
    ring = [(i, (i + 1) % parts) for i in range(parts)]

    def onward(values):
        return lax.ppermute(values, "tensor", ring)

    def gather_ring(own):
        held = [own]
        for _ in range(parts - 1):
            held.append(onward(held[-1]))
        return held

    def scatter_ring(terms):
        total = terms[1 % parts]
        for k in range(2, parts + 1):
            arrived = onward(total.astype(BF16))
            total = arrived.astype(F32) + terms[k % parts]
        return total

    me = lax.axis_index("tensor")
    order = lax.rem(me - jnp.arange(parts, dtype=jnp.int32) + parts, parts)

    w_in = lax.all_gather(jnp.concatenate([input_weight, gelu_weight], axis=1), "dp", axis=0, tiled=True)
    w_mix = lax.all_gather(mixer_weight.T, "dp", axis=0, tiled=True)
    w_ff = lax.all_gather(jnp.concatenate([gate_weight, up_weight], axis=1), "dp", axis=0, tiled=True)
    w_down = lax.all_gather(down_weight.T, "dp", axis=0, tiled=True)

    gain_one = first_gain.astype(F32)
    gain_two = second_gain.astype(F32)
    taps = conv_kernel.astype(F32)
    bias_f = conv_bias.astype(F32)[None, :]
    decay_f = decay_param.astype(F32)
    rate = (RATE_SCALE * jax.nn.softplus(decay_f))[None, :]
    gate_w = jnp.concatenate([block_diagonal(alpha_weight), block_diagonal(update_weight)], axis=1)
    gate_b = jnp.concatenate([alpha_bias, update_bias]).astype(F32)[None, :]
    table = mask_table(segment_ids[0], conv_kernel.shape[0])

    inputs_f = block_input.astype(F32)
    normed = norm_rows(inputs_f, gain_one).astype(BF16)
    normed_blocks = gather_ring(normed)
    bg = jnp.stack([matmul(block, w_in) for block in normed_blocks])
    mixed, states, conv_low = recurrent_forward(order, bg, table, taps, bias_f, gate_w, gate_b, rate)
    mix_terms = [lax.optimization_barrier(times_transposed(mixed[k], w_mix)) for k in range(parts)]
    middle = inputs_f + scatter_ring(mix_terms)
    second = norm_rows(middle, gain_two).astype(BF16)

    cot_blocks = gather_ring(output_cotangent)
    second_blocks = gather_ring(second)
    hidden_blocks, d_ff_blocks = [], []
    for k in range(parts):
        gate_up = matmul(second_blocks[k], w_ff)
        d_hidden = matmul(cot_blocks[k], w_down)
        hidden, hidden_back = jax.vjp(gated_hidden, gate_up[:, :units], gate_up[:, units:])
        d_gate, d_up = hidden_back(d_hidden)
        hidden_blocks.append(hidden.astype(BF16))
        d_ff_blocks.append(jnp.concatenate([d_gate, d_up], axis=1).astype(BF16))
    second_terms = [lax.optimization_barrier(times_transposed(d, w_ff)) for d in d_ff_blocks]
    d_second = scatter_ring(second_terms)
    out_terms = [lax.optimization_barrier(times_transposed(h, w_down)) for h in hidden_blocks]
    block_output = (middle + scatter_ring(out_terms)).astype(BF16)

    cot_all = jnp.concatenate(cot_blocks, axis=0)
    grad_down_t = inner_rows(cot_all, jnp.concatenate(hidden_blocks, axis=0)).astype(BF16)
    grad_ff = inner_rows(
        jnp.concatenate(second_blocks, axis=0), jnp.concatenate(d_ff_blocks, axis=0)
    ).astype(BF16)

    _, norm_two_back = jax.vjp(norm_rows, middle, gain_two)
    d_middle_norm, grad_gain_two = norm_two_back(d_second)
    d_middle = output_cotangent.astype(F32) + d_middle_norm
    d_middle_blocks = gather_ring(d_middle.astype(BF16))
    d_mixed = jnp.stack([matmul(d, w_mix) for d in d_middle_blocks])
    d_bg, grad_gates, sums, bias_sums = recurrent_backward(
        order, d_mixed, bg, states, conv_low, table, taps, gate_w, gate_b, rate
    )
    grad_mix_t = inner_rows(
        jnp.concatenate(d_middle_blocks, axis=0), mixed.reshape(parts * rows, channels)
    ).astype(BF16)
    grad_in = inner_rows(
        jnp.concatenate(normed_blocks, axis=0), d_bg.reshape(parts * rows, 2 * channels)
    ).astype(BF16)
    first_terms = [lax.optimization_barrier(times_transposed(d_bg[k], w_in)) for k in range(parts)]
    d_normed = scatter_ring(first_terms)
    _, norm_one_back = jax.vjp(norm_rows, inputs_f, gain_one)
    d_inputs_norm, grad_gain_one = norm_one_back(d_normed)
    input_grad = d_middle + d_inputs_norm

    def spread(grad):
        return lax.psum_scatter(grad, "dp", scatter_dimension=0, tiled=True).astype(F32)

    own_down = spread(grad_down_t).T
    own_ff = spread(grad_ff)
    own_mix = spread(grad_mix_t).T
    own_in = spread(grad_in)

    sums = jnp.sum(sums, axis=1)
    bias_sums = jnp.sum(bias_sums, axis=0)
    grad_kernel, grad_bias = sums[:4], sums[4]
    grad_decay = -RATE_SCALE * sums[5] * jax.nn.sigmoid(decay_f)

    def diagonal(start):
        return jnp.stack(
            [
                lax.slice(
                    grad_gates,
                    (b * block_width, start + b * block_width),
                    ((b + 1) * block_width, start + (b + 1) * block_width),
                )
                for b in range(blocks)
            ]
        )

    small = lax.psum(
        (
            grad_kernel,
            grad_bias,
            diagonal(0),
            bias_sums[:channels],
            diagonal(channels),
            bias_sums[channels:],
            grad_decay,
        ),
        "dp",
    )
    gains = lax.psum((grad_gain_one, grad_gain_two), ("dp", "tensor"))
    return (
        block_output,
        input_grad,
        gains[0],
        own_in[:, :channels],
        own_in[:, channels:],
        small[0],
        small[1],
        small[2],
        small[3],
        small[4],
        small[5],
        small[6],
        own_mix,
        gains[1],
        own_ff[:, :units],
        own_ff[:, units:],
        own_down,
    )


def solution(mesh):
    in_specs = (
        P(("dp", "tensor"), None),
        P("dp", None),
        P(("dp", "tensor"), None),
        P(),
        P("dp", "tensor"),
        P("dp", "tensor"),
        P(None, "tensor"),
        P("tensor"),
        P("tensor", None, None),
        P("tensor"),
        P("tensor", None, None),
        P("tensor"),
        P("tensor"),
        P("tensor", "dp"),
        P(),
        P("dp", "tensor"),
        P("dp", "tensor"),
        P("tensor", "dp"),
    )
    out_specs = (
        P(("dp", "tensor"), None),
        P(("dp", "tensor"), None),
        P(),
        P("dp", "tensor"),
        P("dp", "tensor"),
        P(None, "tensor"),
        P("tensor"),
        P("tensor", None, None),
        P("tensor"),
        P("tensor", None, None),
        P("tensor"),
        P("tensor"),
        P("tensor", "dp"),
        P(),
        P("dp", "tensor"),
        P("dp", "tensor"),
        P("tensor", "dp"),
    )
    return jax.shard_map(
        partial(body, mesh.shape["tensor"]),
        mesh=mesh,
        in_specs=in_specs,
        out_specs=out_specs,
        check_vma=False,
    )
```
